32 devices in a mesh: segment: 4 (over y, x), expert: 8 (over z, core).
Axes of the slice: x: 2, y: 2, z: 4, core: 2. Of those that a mesh axis runs over, the one named last changes fastest.
Arguments:
- state_up: bfloat16 [4, 64, 3584], P('segment', 'expert'), may hold values from -6 to 6
- state_down: bfloat16 [4, 64, 3584], P('segment', 'expert'), may hold values from -6 to 6
- feed_up: bfloat16 [1, 64, 3584], P(None, 'expert'), may hold values from -6 to 6
- feed_down: bfloat16 [1, 64, 3584], P(None, 'expert'), may hold values from -6 to 6
- routes: int32 [2, 2, 4, 64, 2], P(None, None, 'segment', 'expert'), may hold values from 0 to 7, all different within a row; in each aligned block of 8 rows (0 to 7, 8 to 15, ..., all dimensions but the last counted through in order) at most 2 rows name the same one
- mixing: float32 [2, 2, 4, 64, 2], P(None, None, 'segment', 'expert'), may hold values from 0.2 to 1
- norm_gain: float32 [4, 3584], P('segment'), may hold values from 0.5 to 1.5
- gate_weight: bfloat16 [4, 3584, 8192], P('segment', None, 'expert'), may hold values from -0.09375 to 0.09375
- up_weight: bfloat16 [4, 3584, 8192], P('segment', None, 'expert'), may hold values from -0.09375 to 0.09375
- down_weight: bfloat16 [4, 8192, 3584], P('segment', 'expert'), may hold values from -0.1875 to 0.1875
Outputs:
- final_up: bfloat16 [4, 64, 3584], P('segment', 'expert')
- final_down: bfloat16 [4, 64, 3584], P('segment', 'expert')
The draws below stay inside these ranges and needn't reach their ends.
Inputs may be any that keep to these rules, and one draw needn't show every extreme that they name: `routes`: the 2 experts of a token differ. Within the rows of one device for one step, direction and section, at most 2 name any one expert, a bound that some block reaches.
All inputs are finite; a program needn't handle non-finite values.
Results may differ from the reference program's by a relative error of at most 0.0065.
Values may be sent and summed in bfloat16 or wider, within the bound.
A program may use at most 64 MiB of HBM per device.

```python
import math
import jax
import jax.numpy as jnp
import numpy as np
from jax import lax

D = 3584
FF = 1024
EXPERTS = 8
TOP = 2
TICKS = 2
TOK = 8
CAP = 2
SHARDS = 1
FF_DEV = 1024
TOKENS = 64
N_SEGMENT = 4
N_EXPERT = 8


def levels(rng, extent, shards, low, top_value):
    level = 1.0
    for axis_at, parts in shards:
        heights = jax.random.uniform(jax.random.fold_in(jax.random.fold_in(rng, 6), axis_at), (parts,), jnp.float32, low / len(shards), top_value / len(shards))
        level = level * jnp.repeat(jnp.exp(heights), extent[axis_at] // parts).reshape((-1,) + (1,) * (len(extent) - 1 - axis_at))
    return level


def deal_out(rng, own, number, rows, amount, top, bound, lean):
    order = jax.random.permutation(rng, amount)
    crowded, ordinary = load_shares(amount, rows * top, bound, lean, True), load_shares(amount, rows * top, bound, lean, False)
    places = jnp.arange(amount)

    def named(tallies, rotation):
        used = int((tallies > 0).sum())
        fixed = max(1, used // 4)
        moved = fixed + (places - fixed + rotation * (used - fixed)) % max(1, amount - fixed)
        return jnp.zeros((amount,), jnp.int32).at[order[jnp.where(places < fixed, places, moved)]].set(jnp.asarray(tallies, jnp.int32))

    tallies = jnp.where(number % 4 == 0, named(crowded, number // 4), named(ordinary, number - number // 4 - 1))
    mixed = jax.random.permutation(jax.random.fold_in(own, 3), amount)
    donor, taker = mixed[0:amount // 2 * 2:2], mixed[1:amount // 2 * 2:2]
    slack = jnp.minimum(tallies[donor] - 1, bound - tallies[taker]) // 2
    slack = jnp.where((donor == order[0]) | (taker == order[0]) | (tallies[taker] == 0), 0, jnp.maximum(slack, 0))
    moved = jax.random.randint(jax.random.fold_in(own, 4), (amount // 2,), 0, 1 << 20) % (slack + 1)
    tallies = tallies.at[donor].add(-moved).at[taker].add(moved)
    labels = jnp.searchsorted(jnp.cumsum(tallies), jnp.arange(rows * top), side="right").astype(jnp.int32)
    listing = labels.reshape(top, rows).T
    listing = listing[jax.random.permutation(jax.random.fold_in(own, 1), rows)]
    rotation = jax.random.randint(jax.random.fold_in(own, 2), (rows, 1), 0, top)
    return jnp.take_along_axis(listing, (jnp.arange(top)[None, :] + rotation) % top, axis=1)


def load_shares(amount, total, limit, lean, full):
    portions = [(1 << 20) // math.isqrt(grade ** lean) + 1 for grade in range(1, amount + 1)]
    largest = limit if full else min(limit, max(-(-total // amount), total * portions[0] // sum(portions)))
    least = 1 if total - largest >= amount - 1 else 0
    holding, surplus = [largest] + [least] * (amount - 1), total - largest - least * (amount - 1)
    while surplus > 0:
        free = [i for i in range(1, amount) if holding[i] < largest] or [i for i in range(1, amount) if holding[i] < limit]
        pool, remaining = sum([portions[i] for i in free]), surplus
        for i in free:
            addition = min(limit - holding[i], max(1, remaining * portions[i] // pool), surplus)
            holding[i] = holding[i] + addition
            surplus = surplus - addition
    return np.array(holding)


def noise(rng, extent, width, bound, shards=(), kind=jnp.bfloat16):
    loudness = levels(rng, extent, shards, -0.22, 0.18) if shards else 1.0
    result = jax.random.normal(rng, extent, jnp.float32) * width * loudness
    return jnp.minimum(jnp.maximum(result, -bound), bound).astype(kind)


def setup_inputs(seed: int = 0) -> dict:
    splits = jax.random.split(jax.random.key(seed), 11)
    state_up = noise(splits[0], (N_SEGMENT, TOKENS, D), 1.0, 6.0, ((0, 4), (1, 8)))
    state_down = noise(splits[1], (N_SEGMENT, TOKENS, D), 1.0, 6.0, ((0, 4), (1, 8)))
    feed_up = noise(splits[2], (TICKS - 1, TOKENS, D), 1.0, 6.0, ((1, 8),))
    feed_down = noise(splits[3], (TICKS - 1, TOKENS, D), 1.0, 6.0, ((1, 8),))
    routes_keys = jax.random.split(jax.random.fold_in(splits[4], 1), TICKS * 2 * N_SEGMENT * TOKENS // TOK)
    routes_turns = jax.random.permutation(jax.random.fold_in(splits[4], 3), TICKS * 2 * N_SEGMENT * TOKENS // TOK)
    routes = jax.vmap(lambda own, number: deal_out(jax.random.fold_in(splits[4], 2), own, number, TOK, EXPERTS, TOP, CAP, 0))(routes_keys, routes_turns).reshape((TICKS, 2, N_SEGMENT, TOKENS, TOP))
    mixing = jnp.clip(0.2 + 0.8 * jax.random.uniform(splits[5], (TICKS, 2, N_SEGMENT, TOKENS, TOP), jnp.float32) ** levels(splits[5], (TICKS, 2, N_SEGMENT, TOKENS, TOP), ((2, 4), (3, 8)), -0.2, 0.2), 0.2, 1.0)
    norm_gain = jnp.clip(1.0 + 0.1 * jax.random.normal(splits[6], (N_SEGMENT, D), jnp.float32), 0.5, 1.5)
    gate_weight = noise(splits[7], (N_SEGMENT, D, EXPERTS * FF), D ** -0.5, 0.09375, ((0, 4), (2, 8)))
    up_weight = noise(splits[8], (N_SEGMENT, D, EXPERTS * FF), D ** -0.5, 0.09375, ((0, 4), (2, 8)))
    down_weight = noise(splits[9], (N_SEGMENT, EXPERTS * FF, D), FF ** -0.5, 0.1875, ((0, 4), (1, 8)))
    return {"state_up": state_up, "state_down": state_down, "feed_up": feed_up, "feed_down": feed_down, "routes": routes, "mixing": mixing, "norm_gain": norm_gain, "gate_weight": gate_weight, "up_weight": up_weight, "down_weight": down_weight}


norm_eps = 1e-06

def normed(state, gain_row):
    values = state.astype(jnp.float32)
    inv_scale = lax.rsqrt(lax.optimization_barrier(jnp.mean(values * values, axis=-1, keepdims=True)) + norm_eps)
    return (values * inv_scale * gain_row[None, :]).astype(jnp.bfloat16)

def slot_table(route_rows):
    blocks = route_rows.reshape(N_EXPERT, TOK * TOP)
    onehot = (blocks[:, :, None] == jnp.arange(EXPERTS, dtype=jnp.int32)[None, None, :]).astype(jnp.int32)
    slots = lax.optimization_barrier(jnp.sum(jnp.cumsum(onehot, axis=1) * onehot, axis=2)) - 1
    return slots.reshape(TOKENS * TOP).astype(jnp.int32)

def expert_pass(packed):
    expert_rows, gate_part, up_part, down_part = packed
    gate_val = jnp.dot(expert_rows, gate_part, preferred_element_type=jnp.float32)
    up_val = jnp.dot(expert_rows, up_part, preferred_element_type=jnp.float32)
    hidden = (jax.nn.silu(gate_val) * up_val).astype(jnp.bfloat16)
    total = jnp.zeros((expert_rows.shape[0], D), jnp.float32)
    for shard_index in range(SHARDS):
        lower_col = shard_index * FF_DEV
        piece = jnp.dot(hidden[:, lower_col:lower_col + FF_DEV], down_part[lower_col:lower_col + FF_DEV], preferred_element_type=jnp.float32)
        rounded = lax.optimization_barrier(piece.astype(jnp.bfloat16))
        total = total + rounded.astype(jnp.float32)
    return total

def apply_layer(packed):
    state, route_rows, weight_rows, gain_row, gate_all, up_all, down_all = packed
    normed_rows = normed(state, gain_row)
    flat_expert = route_rows.reshape(-1).astype(jnp.int32)
    slots = slot_table(route_rows)
    entries = jnp.arange(TOKENS * TOP, dtype=jnp.int32)
    source = entries // (TOK * TOP)
    token_index = entries // TOP
    place = (source * CAP + slots).astype(jnp.int32)
    index = jnp.zeros((EXPERTS, N_EXPERT * CAP), jnp.int32).at[flat_expert, place].set(token_index)
    gathered = normed_rows[index]
    gate_split = jnp.transpose(gate_all.reshape(D, EXPERTS, FF), (1, 0, 2))
    up_split = jnp.transpose(up_all.reshape(D, EXPERTS, FF), (1, 0, 2))
    down_split = down_all.reshape(EXPERTS, FF, D)
    outputs = lax.map(expert_pass, (gathered, gate_split, up_split, down_split))
    picked = outputs[flat_expert, place].reshape(TOKENS, TOP, D)
    mixed = lax.optimization_barrier(jnp.sum(picked * weight_rows[:, :, None], axis=1))
    return (state.astype(jnp.float32) + mixed).astype(jnp.bfloat16)

def reference(state_up, state_down, feed_up, feed_down, routes, mixing, norm_gain, gate_weight, up_weight, down_weight):
    upper = state_up
    lower = state_down
    for tick_index in range(TICKS):
        upper = lax.map(apply_layer, (upper, routes[tick_index, 0], mixing[tick_index, 0], norm_gain, gate_weight, up_weight, down_weight))
        lower = lax.map(apply_layer, (lower, routes[tick_index, 1], mixing[tick_index, 1], norm_gain, gate_weight, up_weight, down_weight))
        if tick_index + 1 < TICKS:
            upper = jnp.concatenate([feed_up[tick_index][None], upper[:-1]], axis=0)
            lower = jnp.concatenate([lower[1:], feed_down[tick_index][None]], axis=0)
    return (upper, lower)
```

```python
import functools

import jax
import jax.numpy as jnp
from jax import lax
from jax.experimental import pallas as pl
from jax.experimental.pallas import tpu as pltpu
from jax.sharding import PartitionSpec as P

EXPERTS = 8
TOP = 2
TICKS = 2
CAP = 2
DIRS = 2
LANES = 128
RPB = DIRS * CAP
QUADS = 16 // RPB
SPAN = QUADS * LANES
MESH = pl.DeviceIdType.MESH

norm_eps = 1e-06

RETURN_CUTS = (0, 2, 4, 7)
GATE_TILE = 256


def iota(shape, axis):
    return lax.broadcasted_iota(jnp.int32, shape, axis)


def stack(rows):
    chunks = rows.shape[1] // SPAN
    return jnp.concatenate(
        [
            jnp.concatenate(
                [rows[:, c * SPAN + q * LANES : c * SPAN + (q + 1) * LANES] for c in range(chunks)],
                axis=1,
            )
            for q in range(QUADS)
        ],
        axis=0,
    )


def unstack(rows, count):
    return jnp.concatenate(
        [
            rows[q * count : (q + 1) * count, c * LANES : (c + 1) * LANES]
            for c in range(rows.shape[1] // LANES)
            for q in range(QUADS)
        ],
        axis=1,
    )


def one_hot(condition):
    return jnp.where(condition, 1.0, 0.0).astype(jnp.bfloat16)


def select(matrix, rows):
    return jnp.dot(matrix, rows, preferred_element_type=jnp.float32)


def tables(routes, tokens):
    wide = DIRS * QUADS * tokens
    blocks = EXPERTS * 16
    eye = iota((tokens, LANES), 0) == iota((tokens, LANES), 1)
    before = iota((tokens, LANES), 1) < iota((tokens, LANES), 0)
    columns = [[] for _ in range(TOP)]
    for rows in routes:
        cols = [rows[:, k : k + 1] for k in range(TOP)]
        lying = [jnp.sum(jnp.where(eye, c, 0), axis=0, keepdims=True) for c in cols]
        for k in range(TOP):
            same = sum(jnp.where(before & (cols[k] == line), 1, 0) for line in lying)
            place = cols[k] * CAP + jnp.sum(same, axis=1, keepdims=True)
            columns[k] += [place] * QUADS
    columns = [jnp.concatenate(c, axis=0) for c in columns]
    big_eye = iota((wide, wide), 0) == iota((wide, wide), 1)
    i, j = iota((blocks, wide), 0), iota((blocks, wide), 1)
    slot = (i // 16) * CAP + i % CAP
    fits = ((i // CAP) % DIRS == j // (QUADS * tokens)) & (
        (i // RPB) % QUADS == (j // tokens) % QUADS
    )
    named = False
    for c in columns:
        named = named | (slot == jnp.sum(jnp.where(big_eye, c, 0), axis=0, keepdims=True))
    pack = one_hot(fits & named)
    i, j = iota((wide, blocks), 1), iota((wide, blocks), 0)
    slot = (i // 16) * CAP + i % CAP
    fits = ((i // CAP) % DIRS == j // (QUADS * tokens)) & (
        (i // RPB) % QUADS == (j // tokens) % QUADS
    )
    picks = [one_hot(fits & (slot == c)) for c in columns]
    return pack, jnp.concatenate(picks, axis=0)


def kernel(
    n,
    ns,
    up_ref,
    down_ref,
    feed_up_ref,
    feed_down_ref,
    routes_ref,
    mixing_ref,
    gain_ref,
    gate_hbm,
    upw_hbm,
    downw_hbm,
    out_up_ref,
    out_down_ref,
    gate_v,
    upw_v,
    downw_v,
    send_buf,
    recv_buf,
    back_buf,
    ret_buf,
    rows_buf,
    hidden_buf,
    move_src,
    move_dst,
    w_sem,
    d_send,
    d_recv,
    r_send,
    r_recv,
    m_send,
    m_recv,
):
    me = lax.axis_index("expert")
    seg = lax.axis_index("segment")
    shards = n // EXPERTS
    tokens = up_ref.shape[1]
    width = up_ref.shape[2]
    ff = gate_v.shape[1]
    tile = min(GATE_TILE, ff)
    cols = width // QUADS
    group_rows = EXPERTS * RPB

    w_copies = []
    for f in range(ff // tile):
        for hbm, vmem in ((gate_hbm, gate_v), (upw_hbm, upw_v)):
            at = pl.ds(f * tile, tile)
            w_copies.append(
                pltpu.make_async_copy(hbm.at[0, :, at], vmem.at[:, at], w_sem.at[len(w_copies)])
            )
    gate_copies = len(w_copies)
    for a, b in zip(RETURN_CUTS[:-1], RETURN_CUTS[1:]):
        at = pl.ds(a * SPAN, (b - a) * SPAN)
        w_copies.append(
            pltpu.make_async_copy(downw_hbm.at[0, :, at], downw_v.at[:, at], w_sem.at[len(w_copies)])
        )
    for copy in w_copies:
        copy.start()

    barrier = pltpu.get_barrier_semaphore()
    for step in range(1, n):
        pl.semaphore_signal(
            barrier, inc=1, device_id={"expert": lax.rem(me + step, n)}, device_id_type=MESH
        )
    for step in (1, ns - 1):
        pl.semaphore_signal(
            barrier, inc=1, device_id={"segment": lax.rem(seg + step, ns)}, device_id_type=MESH
        )

    gain = gain_ref[...]
    gain_lines = [
        jnp.concatenate(
            [gain[:, c * SPAN + q * LANES : c * SPAN + (q + 1) * LANES] for c in range(width // SPAN)],
            axis=1,
        )
        for q in range(QUADS)
    ]
    gain_wide = jnp.concatenate(
        [jnp.broadcast_to(line, (tokens, cols)) for line in gain_lines], axis=0
    )

    size = QUADS * group_rows
    a, b = iota((size, size), 0), iota((size, size), 1)
    unscramble = one_hot(
        ((a // RPB) % EXPERTS == b // 16)
        & (a // group_rows == (b // RPB) % QUADS)
        & (a % RPB == b % RPB)
    )
    a, b = b, a
    scramble = one_hot(
        ((a // RPB) % EXPERTS == b // 16)
        & (a // group_rows == (b // RPB) % QUADS)
        & (a % RPB == b % RPB)
    )

    def normed(values):
        squares = jnp.sum(values * values, axis=1, keepdims=True)
        total = sum(squares[q * tokens : (q + 1) * tokens] for q in range(QUADS))
        inv = lax.rsqrt(total / width + norm_eps)
        inv = jnp.concatenate([inv] * QUADS, axis=0)
        return values * inv * gain_wide

    state = [
        stack(up_ref[0].astype(jnp.float32)),
        stack(down_ref[0].astype(jnp.float32)),
    ]
    pending = []
    for tick in range(TICKS):
        pack, pick = tables([routes_ref[tick, d, 0] for d in range(DIRS)], tokens)
        rows = jnp.concatenate([normed(s) for s in state], axis=0).astype(jnp.bfloat16)
        packed = select(pack, rows).astype(jnp.bfloat16)
        send_buf[tick] = packed.reshape(EXPERTS, 16, cols)
        if tick == 0:
            pl.semaphore_wait(barrier, n + 1)

        for step in range(1, n):
            dest = lax.rem(me + step, n)
            copy = pltpu.make_async_remote_copy(
                src_ref=send_buf.at[tick, dest // shards],
                dst_ref=recv_buf.at[tick, me],
                send_sem=d_send.at[tick, step],
                recv_sem=d_recv.at[tick, me],
                device_id={"expert": dest},
                device_id_type=MESH,
            )
            copy.start()
            pending.append(copy)
        recv_buf[tick, me] = send_buf[tick, me // shards]

        for step in range(1, n):
            source = lax.rem(me + n - step, n)
            pltpu.make_async_remote_copy(
                src_ref=send_buf.at[tick, 0],
                dst_ref=recv_buf.at[tick, source],
                send_sem=d_send.at[tick, step],
                recv_sem=d_recv.at[tick, source],
                device_id={"expert": source},
                device_id_type=MESH,
            ).wait_recv()

        for g in range(n // EXPERTS):
            block = recv_buf[tick, g * EXPERTS : (g + 1) * EXPERTS].reshape(EXPERTS * 16, cols)
            straight = select(unscramble, block)
            rows_buf[g * group_rows : (g + 1) * group_rows, :] = unstack(
                straight, group_rows
            ).astype(jnp.bfloat16)

        lhs = rows_buf[...]
        for f in range(ff // tile):
            if tick == 0:
                w_copies[2 * f].wait()
                w_copies[2 * f + 1].wait()
            at = slice(f * tile, (f + 1) * tile)
            gate = jnp.dot(lhs, gate_v[:, at], preferred_element_type=jnp.float32)
            up = jnp.dot(lhs, upw_v[:, at], preferred_element_type=jnp.float32)
            hidden_buf[:, at] = (jax.nn.silu(gate) * up).astype(jnp.bfloat16)

        hidden = hidden_buf[...]
        my_place = lax.rem(me, shards) * EXPERTS + me // shards
        for r, (lo, hi) in enumerate(zip(RETURN_CUTS[:-1], RETURN_CUTS[1:])):
            if tick == 0:
                w_copies[gate_copies + r].wait()
            piece = jnp.dot(
                hidden, downw_v[:, lo * SPAN : hi * SPAN], preferred_element_type=jnp.float32
            )
            for g in range(n // EXPERTS):
                part = stack(piece[g * group_rows : (g + 1) * group_rows]).astype(jnp.bfloat16)
                block = select(scramble, part).astype(jnp.bfloat16)
                back_buf[tick, g * EXPERTS : (g + 1) * EXPERTS, :, lo * LANES : hi * LANES] = (
                    block.reshape(EXPERTS, 16, (hi - lo) * LANES)
                )
            at = pl.ds(lo * LANES, (hi - lo) * LANES)
            for step in range(1, n):
                dest = lax.rem(me + step, n)
                copy = pltpu.make_async_remote_copy(
                    src_ref=back_buf.at[tick, dest, :, at],
                    dst_ref=ret_buf.at[tick, my_place, :, at],
                    send_sem=r_send.at[tick, r, step],
                    recv_sem=r_recv.at[tick, r, my_place],
                    device_id={"expert": dest},
                    device_id_type=MESH,
                )
                copy.start()
                pending.append(copy)
            ret_buf[tick, my_place, :, lo * LANES : hi * LANES] = back_buf[
                tick, me, :, lo * LANES : hi * LANES
            ]

        weights = []
        for k in range(TOP):
            pieces = []
            for d in range(DIRS):
                pieces += [mixing_ref[tick, d, 0][:, k : k + 1]] * QUADS
            weights.append(jnp.concatenate(pieces, axis=0))
        old = jnp.concatenate(state, axis=0)
        wide = old.shape[0]
        results = []
        for r, (lo, hi) in enumerate(zip(RETURN_CUTS[:-1], RETURN_CUTS[1:])):
            at = pl.ds(lo * LANES, (hi - lo) * LANES)
            for step in range(1, n):
                source = lax.rem(me + n - step, n)
                place = lax.rem(source, shards) * EXPERTS + source // shards
                pltpu.make_async_remote_copy(
                    src_ref=back_buf.at[tick, 0, :, at],
                    dst_ref=ret_buf.at[tick, place, :, at],
                    send_sem=r_send.at[tick, r, step],
                    recv_sem=r_recv.at[tick, r, place],
                    device_id={"expert": source},
                    device_id_type=MESH,
                ).wait_recv()
            total = None
            for s in range(shards):
                block = ret_buf[
                    tick, s * EXPERTS : (s + 1) * EXPERTS, :, lo * LANES : hi * LANES
                ].reshape(EXPERTS * 16, (hi - lo) * LANES)
                found = select(pick, block)
                total = found if total is None else total + found
            mixed = total[:wide] * weights[0] + total[wide:] * weights[1]
            results.append(old[:, lo * LANES : hi * LANES] + mixed)
        result = jnp.concatenate(results, axis=1)
        half = QUADS * tokens
        halves = [result[:half], result[half:]]

        if tick + 1 < TICKS:
            state = []
            for d, (feed_ref, ahead) in enumerate(((feed_up_ref, 1), (feed_down_ref, ns - 1))):
                edge_out = ns - 1 if d == 0 else 0
                edge_in = 0 if d == 0 else ns - 1
                move_src[tick, d] = halves[d].astype(jnp.bfloat16)
                copy = pltpu.make_async_remote_copy(
                    src_ref=move_src.at[tick, d],
                    dst_ref=move_dst.at[tick, d],
                    send_sem=m_send.at[tick, d],
                    recv_sem=m_recv.at[tick, d],
                    device_id={"segment": lax.rem(seg + ahead, ns)},
                    device_id_type=MESH,
                )

                @pl.when(seg != edge_out)
                def _():
                    copy.start()

                @pl.when(seg == edge_in)
                def _():
                    move_dst[tick, d] = stack(feed_ref[tick].astype(jnp.float32)).astype(
                        jnp.bfloat16
                    )

                state.append((copy, edge_in, edge_out))
            moves = state
            state = []
            for d, (copy, edge_in, edge_out) in enumerate(moves):

                @pl.when(seg != edge_in)
                def _():
                    copy.wait_recv()

                state.append(move_dst[tick, d].astype(jnp.float32))
            for d, (copy, edge_in, edge_out) in enumerate(moves):

                @pl.when(seg != edge_out)
                def _():
                    copy.wait_send()
        else:
            out_up_ref[0] = unstack(halves[0], tokens).astype(jnp.bfloat16)
            out_down_ref[0] = unstack(halves[1], tokens).astype(jnp.bfloat16)

    for copy in pending:
        copy.wait_send()


def body(
    state_up,
    state_down,
    feed_up,
    feed_down,
    routes,
    mixing,
    norm_gain,
    gate_weight,
    up_weight,
    down_weight,
):
    n = lax.axis_size("expert")
    ns = lax.axis_size("segment")
    _, tokens, width = state_up.shape
    ff = gate_weight.shape[2]
    tile = min(GATE_TILE, ff)
    cols = width // QUADS
    parts = len(RETURN_CUTS) - 1
    bf16 = jnp.bfloat16
    vmem = pl.BlockSpec(memory_space=pltpu.VMEM)
    hbm = pl.BlockSpec(memory_space=pl.ANY)
    dma = pltpu.SemaphoreType.DMA
    return pl.pallas_call(
        functools.partial(kernel, n, ns),
        out_shape=(
            jax.ShapeDtypeStruct(state_up.shape, bf16),
            jax.ShapeDtypeStruct(state_down.shape, bf16),
        ),
        in_specs=[vmem] * 7 + [hbm] * 3,
        out_specs=(vmem, vmem),
        scratch_shapes=[
            pltpu.VMEM((width, ff), bf16),
            pltpu.VMEM((width, ff), bf16),
            pltpu.VMEM((ff, width), bf16),
            pltpu.VMEM((TICKS, EXPERTS, 16, cols), bf16),
            pltpu.VMEM((TICKS, n, 16, cols), bf16),
            pltpu.VMEM((TICKS, n, 16, cols), bf16),
            pltpu.VMEM((TICKS, n, 16, cols), bf16),
            pltpu.VMEM((n * RPB, width), bf16),
            pltpu.VMEM((n * RPB, ff), bf16),
            pltpu.VMEM((TICKS, DIRS, QUADS * tokens, cols), bf16),
            pltpu.VMEM((TICKS, DIRS, QUADS * tokens, cols), bf16),
            dma((2 * (ff // tile) + parts,)),
            dma((TICKS, n)),
            dma((TICKS, n)),
            dma((TICKS, parts, n)),
            dma((TICKS, parts, n)),
            dma((TICKS, DIRS)),
            dma((TICKS, DIRS)),
        ],
        compiler_params=pltpu.CompilerParams(collective_id=0, has_side_effects=True),
    )(
        state_up,
        state_down,
        feed_up,
        feed_down,
        routes,
        mixing,
        norm_gain,
        gate_weight,
        up_weight,
        down_weight,
    )


def solution(mesh):
    placed = (
        P("segment", "expert", None),
        P("segment", "expert", None),
        P(None, "expert", None),
        P(None, "expert", None),
        P(None, None, "segment", "expert", None),
        P(None, None, "segment", "expert", None),
        P("segment", None),
        P("segment", None, "expert"),
        P("segment", None, "expert"),
        P("segment", "expert", None),
    )
    return jax.shard_map(
        body,
        mesh=mesh,
        in_specs=placed,
        out_specs=(P("segment", "expert", None), P("segment", "expert", None)),
        check_vma=False,
    )
```

```python
import functools

import jax
import jax.numpy as jnp
from jax import lax
from jax.experimental import pallas as pl
from jax.experimental.pallas import tpu as pltpu
from jax.sharding import PartitionSpec as P

EXPERTS = 8
TOP = 2
TICKS = 2
CAP = 2
DIRS = 2
LANES = 128
QUADS = 4
ROWS = QUADS * CAP
SPAN = QUADS * LANES
MESH = pl.DeviceIdType.MESH

norm_eps = 1e-06

SEND_CUTS = (0, 3, 7)
RETURN_CUTS = (0, 2, 4, 7)
GATE_TILE = 256


def spans(cuts):
    return list(zip(cuts[:-1], cuts[1:]))


def iota(shape, axis):
    return lax.broadcasted_iota(jnp.int32, shape, axis)


def over(x, k):
    return x >> (k.bit_length() - 1) if k & (k - 1) == 0 else x // k


def mod(x, k):
    return x & (k - 1) if k & (k - 1) == 0 else x % k


def lane_group(rows, q):
    chunks = rows.shape[1] // SPAN
    return jnp.concatenate(
        [rows[:, c * SPAN + q * LANES : c * SPAN + (q + 1) * LANES] for c in range(chunks)], axis=1
    )


def stack(rows):
    return jnp.concatenate([lane_group(rows, q) for q in range(QUADS)], axis=0)


def interleave(groups):
    return jnp.concatenate(
        [
            group[:, c * LANES : (c + 1) * LANES]
            for c in range(groups[0].shape[1] // LANES)
            for group in groups
        ],
        axis=1,
    )


def unstack(rows, count):
    return interleave([rows[q * count : (q + 1) * count] for q in range(QUADS)])


def swap_pairs(parts):
    row = iota(parts[0].shape, 0)
    size = parts[0].shape[0]
    low = mod(row, 8) < 4
    halves = []
    for a, b in ((parts[0], parts[2]), (parts[1], parts[3])):
        halves.append(
            (
                jnp.where(low, a, pltpu.roll(b, 4, 0)),
                jnp.where(low, pltpu.roll(a, size - 4, 0), b),
            )
        )
    low = mod(row, 4) < 2
    result = []
    for side in range(2):
        a, b = halves[0][side], halves[1][side]
        result.append(jnp.where(low, a, pltpu.roll(b, 2, 0)))
        result.append(jnp.where(low, pltpu.roll(a, size - 2, 0), b))
    return result


def one_hot(condition):
    return jnp.where(condition, 1.0, 0.0).astype(jnp.bfloat16)


def select(matrix, rows):
    return jnp.dot(matrix, rows, preferred_element_type=jnp.float32)


def upright(line):
    count = line.shape[1]
    eye = iota((count, count), 0) == iota((count, count), 1)
    return jnp.sum(jnp.where(eye, line, jnp.zeros_like(line)), axis=1, keepdims=True)


def places(rows):
    tokens = rows.shape[1]
    before = iota((tokens, tokens), 1) < iota((tokens, tokens), 0)
    lying = [rows[k : k + 1, :] for k in range(TOP)]
    columns = []
    for k in range(TOP):
        col = upright(lying[k])
        same = sum(jnp.where(before & (col == line), 1, 0) for line in lying)
        place = col * CAP + jnp.sum(same, axis=1, keepdims=True)
        columns.append(jnp.concatenate([place] * QUADS, axis=0))
    return columns


def matching(shape, block_axis, tokens):
    i, j = iota(shape, block_axis), iota(shape, 1 - block_axis)
    slot = over(i, ROWS) * CAP + mod(i, CAP)
    return slot, mod(over(i, CAP), QUADS) == over(j, tokens)


def pack_matrix(columns, tokens):
    wide = QUADS * tokens
    eye = iota((wide, wide), 0) == iota((wide, wide), 1)
    slot, fits = matching((EXPERTS * ROWS, wide), 0, tokens)
    named = False
    for c in columns:
        named = named | (slot == jnp.sum(jnp.where(eye, c, 0), axis=0, keepdims=True))
    return one_hot(fits & named)


def pick_matrix(columns, tokens):
    slot, fits = matching((QUADS * tokens, EXPERTS * ROWS), 1, tokens)
    return jnp.concatenate([one_hot(fits & (slot == c)) for c in columns], axis=0)


def weight_columns(rows):
    return [jnp.concatenate([upright(rows[k : k + 1, :])] * QUADS, axis=0) for k in range(TOP)]


def kernel(
    n,
    ns,
    up_ref,
    down_ref,
    feed_up_ref,
    feed_down_ref,
    routes_ref,
    mixing_ref,
    gain_ref,
    gate_hbm,
    upw_hbm,
    downw_hbm,
    out_ref,
    gate_v,
    upw_v,
    downw_v,
    send_buf,
    recv_buf,
    back_buf,
    ret_buf,
    gate_acc,
    up_acc,
    x_in,
    routes_in,
    mixing_in,
    w_sem,
    d_send,
    d_recv,
    r_send,
    r_recv,
    m_send,
    m_recv,
):
    me = lax.axis_index("expert")
    seg = lax.axis_index("segment")
    shards = n // EXPERTS
    tokens = up_ref.shape[1]
    width = up_ref.shape[2]
    ff = gate_v.shape[1]
    tile = min(GATE_TILE, ff)
    cols = width // QUADS
    quads = n // 4
    state_refs = (up_ref, down_ref)
    feed_refs = (feed_up_ref, feed_down_ref)
    send_spans, return_spans = spans(SEND_CUTS), spans(RETURN_CUTS)

    barrier = pltpu.get_barrier_semaphore()
    for step in range(1, n):
        pl.semaphore_signal(
            barrier, inc=1, device_id={"expert": lax.rem(me + step, n)}, device_id_type=MESH
        )
    for step in (1, ns - 1):
        pl.semaphore_signal(
            barrier, inc=1, device_id={"segment": lax.rem(seg + step, ns)}, device_id_type=MESH
        )

    w_copies = []
    for lo, hi in send_spans:
        for hbm, vmem in ((gate_hbm, gate_v), (upw_hbm, upw_v)):
            at = pl.ds(lo * SPAN, (hi - lo) * SPAN)
            w_copies.append(
                pltpu.make_async_copy(hbm.at[0, at, :], vmem.at[at, :], w_sem.at[len(w_copies)])
            )
    gate_copies = len(w_copies)
    for lo, hi in return_spans:
        at = pl.ds(lo * SPAN, (hi - lo) * SPAN)
        w_copies.append(
            pltpu.make_async_copy(downw_hbm.at[0, :, at], downw_v.at[:, at], w_sem.at[len(w_copies)])
        )
    for copy in w_copies:
        copy.start()

    gain = gain_ref[...]
    gain_wide = jnp.concatenate(
        [jnp.broadcast_to(lane_group(gain, q), (tokens, cols)) for q in range(QUADS)], axis=0
    )

    def normed(values):
        squares = jnp.sum(values * values, axis=1, keepdims=True)
        total = sum(squares[q * tokens : (q + 1) * tokens] for q in range(QUADS))
        inv = lax.rsqrt(total / width + norm_eps)
        inv = jnp.concatenate([inv] * QUADS, axis=0)
        return (values * inv * gain_wide).astype(jnp.bfloat16)

    def edges(d):
        return (ns - 1, 0) if d == 0 else (0, ns - 1)

    state = [stack(ref[0].astype(jnp.float32)) for ref in state_refs]
    packs = [pack_matrix(places(routes_ref[0, d, 0]), tokens) for d in range(DIRS)]
    pending = []
    moved = []
    my_place = lax.rem(me, shards) * EXPERTS + me // shards
    for tick in range(TICKS):
        last = tick + 1 == TICKS
        for d in range(DIRS):
            packed = select(packs[d], normed(state[d]))
            for e in range(EXPERTS):
                send_buf[tick, e, d] = packed[e * ROWS : (e + 1) * ROWS].astype(jnp.bfloat16)
        if tick == 0:
            pl.semaphore_wait(barrier, n + 1)

        for g, (lo, hi) in enumerate(send_spans):
            at = pl.ds(lo * LANES, (hi - lo) * LANES)
            for step in range(1, n):
                dest = lax.rem(me + step, n)
                copy = pltpu.make_async_remote_copy(
                    src_ref=send_buf.at[tick, dest // shards, :, :, at],
                    dst_ref=recv_buf.at[tick, me, :, :, at],
                    send_sem=d_send.at[tick, g, step],
                    recv_sem=d_recv.at[tick, g, me],
                    device_id={"expert": dest},
                    device_id_type=MESH,
                )
                copy.start()
                pending.append(copy)
        recv_buf[tick, me] = send_buf[tick, me // shards]

        if not last:
            for d in range(DIRS):
                edge_out, edge_in = edges(d)
                ahead = 1 if d == 0 else ns - 1
                sources = (state_refs[d].at[0], routes_ref.at[tick, d, 0], mixing_ref.at[tick, d, 0])
                for a, (source, target) in enumerate(zip(sources, (x_in, routes_in, mixing_in))):
                    copy = pltpu.make_async_remote_copy(
                        src_ref=source,
                        dst_ref=target.at[d],
                        send_sem=m_send.at[d, a],
                        recv_sem=m_recv.at[d, a],
                        device_id={"segment": lax.rem(seg + ahead, ns)},
                        device_id_type=MESH,
                    )

                    @pl.when(seg != edge_out)
                    def _():
                        copy.start()

                    moved.append((copy, edge_out, edge_in))

                @pl.when(seg == edge_in)
                def _():
                    x_in[d] = feed_refs[d][tick]
                    routes_in[d] = routes_ref[tick, d, 0]
                    mixing_in[d] = mixing_ref[tick, d, 0]

            packs = [pack_matrix(places(routes_ref[tick + 1, d, 0]), tokens) for d in range(DIRS)]
        else:
            picks = [pick_matrix(places(routes_ref[tick, d, 0]), tokens) for d in range(DIRS)]
            weights = [weight_columns(mixing_ref[tick, d, 0]) for d in range(DIRS)]

        for g, (lo, hi) in enumerate(send_spans):
            at = pl.ds(lo * LANES, (hi - lo) * LANES)
            for step in range(1, n):
                source = lax.rem(me + n - step, n)
                pltpu.make_async_remote_copy(
                    src_ref=send_buf.at[tick, 0, :, :, at],
                    dst_ref=recv_buf.at[tick, source, :, :, at],
                    send_sem=d_send.at[tick, g, step],
                    recv_sem=d_recv.at[tick, g, source],
                    device_id={"expert": source},
                    device_id_type=MESH,
                ).wait_recv()
            parts = [
                jnp.concatenate(
                    [
                        recv_buf[tick, 4 * i + j, d, :, lo * LANES : hi * LANES].astype(jnp.float32)
                        for d in range(DIRS)
                        for i in range(quads)
                    ],
                    axis=0,
                )
                for j in range(4)
            ]
            lhs = interleave([p.astype(jnp.bfloat16) for p in swap_pairs(parts)])
            if tick == 0:
                w_copies[2 * g].wait()
                w_copies[2 * g + 1].wait()
            for f in range(ff // tile):
                at = slice(f * tile, (f + 1) * tile)
                deep = slice(lo * SPAN, hi * SPAN)
                for weight, acc in ((gate_v, gate_acc), (upw_v, up_acc)):
                    value = jnp.dot(lhs, weight[deep, at], preferred_element_type=jnp.float32)
                    if g:
                        value = acc[:, at] + value
                    acc[:, at] = value
        hidden = (jax.nn.silu(gate_acc[...]) * up_acc[...]).astype(jnp.bfloat16)

        for r, (lo, hi) in enumerate(return_spans):
            if tick == 0:
                w_copies[gate_copies + r].wait()
            piece = jnp.dot(
                hidden, downw_v[:, lo * SPAN : hi * SPAN], preferred_element_type=jnp.float32
            )
            parts = swap_pairs([lane_group(piece, q) for q in range(QUADS)])
            for j in range(4):
                for d in range(DIRS):
                    for i in range(quads):
                        row = (d * quads + i) * 8
                        back_buf[tick, 4 * i + j, d, :, lo * LANES : hi * LANES] = parts[j][
                            row : row + 8
                        ].astype(jnp.bfloat16)
            at = pl.ds(lo * LANES, (hi - lo) * LANES)
            if last:
                for step in range(1, n):
                    dest = lax.rem(me + step, n)
                    copy = pltpu.make_async_remote_copy(
                        src_ref=back_buf.at[tick, dest, :, :, at],
                        dst_ref=ret_buf.at[tick, my_place, :, :, at],
                        send_sem=r_send.at[tick, r, 0, step],
                        recv_sem=r_recv.at[tick, r, 0, my_place],
                        device_id={"expert": dest},
                        device_id_type=MESH,
                    )
                    copy.start()
                    pending.append(copy)
                ret_buf[tick, my_place, :, :, lo * LANES : hi * LANES] = back_buf[
                    tick, me, :, :, lo * LANES : hi * LANES
                ]
            else:
                for d in range(DIRS):
                    edge_out, edge_in = edges(d)
                    ahead = 1 if d == 0 else ns - 1
                    batch = []
                    for step in range(n):
                        dest = lax.rem(me + step, n)
                        copy = pltpu.make_async_remote_copy(
                            src_ref=back_buf.at[tick, dest, d, :, at],
                            dst_ref=ret_buf.at[tick, my_place, d, :, at],
                            send_sem=r_send.at[tick, r, d, step],
                            recv_sem=r_recv.at[tick, r, d, my_place],
                            device_id={"segment": lax.rem(seg + ahead, ns), "expert": dest},
                            device_id_type=MESH,
                        )
                        batch.append(copy)
                        moved.append((copy, edge_out, None))

                    @pl.when(seg != edge_out)
                    def _():
                        for copy in batch:
                            copy.start()

        if not last:
            for d in range(DIRS):

                @pl.when(seg != edges(d)[1])
                def _():
                    for copy, edge_out, edge_in in moved:
                        if edge_in == edges(d)[1]:
                            copy.wait_recv()

            picks = [pick_matrix(places(routes_in[d]), tokens) for d in range(DIRS)]
            weights = [weight_columns(mixing_in[d]) for d in range(DIRS)]
            state = [stack(x_in[d].astype(jnp.float32)) for d in range(DIRS)]

        results = [[] for _ in range(DIRS)]
        for r, (lo, hi) in enumerate(return_spans):
            at = pl.ds(lo * LANES, (hi - lo) * LANES)

            def arrived(d, step):
                source = lax.rem(me + n - step, n)
                place = lax.rem(source, shards) * EXPERTS + source // shards
                which = slice(None) if last else d
                pltpu.make_async_remote_copy(
                    src_ref=back_buf.at[tick, 0, which, :, at],
                    dst_ref=ret_buf.at[tick, place, which, :, at],
                    send_sem=r_send.at[tick, r, d, step],
                    recv_sem=r_recv.at[tick, r, d, place],
                    device_id={"expert": source},
                    device_id_type=MESH,
                ).wait_recv()

            if last:
                for step in range(1, n):
                    arrived(0, step)
            else:
                for d in range(DIRS):

                    @pl.when(seg != edges(d)[1])
                    def _():
                        for step in range(n):
                            arrived(d, step)

            for d in range(DIRS):
                total = None
                for s in range(shards):
                    block = jnp.concatenate(
                        [
                            ret_buf[tick, s * EXPERTS + e, d, :, lo * LANES : hi * LANES].astype(
                                jnp.float32
                            )
                            for e in range(EXPERTS)
                        ],
                        axis=0,
                    )
                    if not last:
                        block = jnp.where(seg == edges(d)[1], 0.0, block)
                    found = select(picks[d], block.astype(jnp.bfloat16))
                    total = found if total is None else total + found
                wide = QUADS * tokens
                mixed = total[:wide] * weights[d][0] + total[wide:] * weights[d][1]
                old = state[d][:, lo * LANES : hi * LANES]
                results[d].append(old + mixed)
        state = [jnp.concatenate(r, axis=1).astype(jnp.bfloat16) for r in results]
        if last:
            for d in range(DIRS):
                out_ref[d] = unstack(state[d].astype(jnp.float32), tokens).astype(jnp.bfloat16)
        else:
            state = [s.astype(jnp.float32) for s in state]

    for copy in pending:
        copy.wait_send()
    for d in range(DIRS):

        @pl.when(seg != edges(d)[0])
        def _():
            for copy, edge_out, _ in moved:
                if edge_out == edges(d)[0]:
                    copy.wait_send()


def body(
    state_up,
    state_down,
    feed_up,
    feed_down,
    routes,
    mixing,
    norm_gain,
    gate_weight,
    up_weight,
    down_weight,
):
    n = lax.axis_size("expert")
    ns = lax.axis_size("segment")
    _, tokens, width = state_up.shape
    ff = gate_weight.shape[2]
    cols = width // QUADS
    sends, parts = len(SEND_CUTS) - 1, len(RETURN_CUTS) - 1
    bf16 = jnp.bfloat16
    vmem = pl.BlockSpec(memory_space=pltpu.VMEM)
    hbm = pl.BlockSpec(memory_space=pl.ANY)
    dma = pltpu.SemaphoreType.DMA
    both = pl.pallas_call(
        functools.partial(kernel, n, ns),
        out_shape=jax.ShapeDtypeStruct((DIRS, tokens, width), bf16),
        in_specs=[vmem] * 7 + [hbm] * 3,
        out_specs=vmem,
        scratch_shapes=[
            pltpu.VMEM((width, ff), bf16),
            pltpu.VMEM((width, ff), bf16),
            pltpu.VMEM((ff, width), bf16),
            pltpu.VMEM((TICKS, EXPERTS, DIRS, ROWS, cols), bf16),
            pltpu.VMEM((TICKS, n, DIRS, ROWS, cols), bf16),
            pltpu.VMEM((TICKS, n, DIRS, ROWS, cols), bf16),
            pltpu.VMEM((TICKS, n, DIRS, ROWS, cols), bf16),
            pltpu.VMEM((n * DIRS * CAP, ff), jnp.float32),
            pltpu.VMEM((n * DIRS * CAP, ff), jnp.float32),
            pltpu.VMEM((DIRS, tokens, width), bf16),
            pltpu.VMEM((DIRS, TOP, tokens), jnp.int32),
            pltpu.VMEM((DIRS, TOP, tokens), jnp.float32),
            dma((2 * sends + parts,)),
            dma((TICKS, sends, n)),
            dma((TICKS, sends, n)),
            dma((TICKS, parts, DIRS, n)),
            dma((TICKS, parts, DIRS, n)),
            dma((DIRS, 3)),
            dma((DIRS, 3)),
        ],
        compiler_params=pltpu.CompilerParams(collective_id=0, has_side_effects=True),
    )(
        state_up,
        state_down,
        feed_up,
        feed_down,
        jnp.swapaxes(routes, 3, 4),
        jnp.swapaxes(mixing, 3, 4),
        norm_gain,
        gate_weight,
        up_weight,
        down_weight,
    )
    return both[0:1], both[1:2]


def solution(mesh):
    placed = (
        P("segment", "expert", None),
        P("segment", "expert", None),
        P(None, "expert", None),
        P(None, "expert", None),
        P(None, None, "segment", "expert", None),
        P(None, None, "segment", "expert", None),
        P("segment", None),
        P("segment", None, "expert"),
        P("segment", None, "expert"),
        P("segment", "expert", None),
    )
    return jax.shard_map(
        body,
        mesh=mesh,
        in_specs=placed,
        out_specs=(P("segment", "expert", None), P("segment", "expert", None)),
        check_vma=False,
    )
```

```python
import functools

import jax
import jax.numpy as jnp
from jax import lax
from jax.experimental import pallas as pl
from jax.experimental.pallas import tpu as pltpu
from jax.sharding import PartitionSpec as P

EXPERTS = 8
TOP = 2
TICKS = 2
CAP = 2
DIRS = 2
LANES = 128
QUADS = 4
ROWS = QUADS * CAP
SPAN = QUADS * LANES
MESH = pl.DeviceIdType.MESH

norm_eps = 1e-06

SEND_CUTS = (0, 3, 7)
RETURN_CUTS = (0, 3, 7)
GATE_TILE = 256


def spans(cuts):
    return list(zip(cuts[:-1], cuts[1:]))


def iota(shape, axis):
    return lax.broadcasted_iota(jnp.int32, shape, axis)


def over(x, k):
    return x >> (k.bit_length() - 1) if k & (k - 1) == 0 else x // k


def mod(x, k):
    return x & (k - 1) if k & (k - 1) == 0 else x % k


def lane_group(rows, q):
    chunks = rows.shape[1] // SPAN
    return jnp.concatenate(
        [rows[:, c * SPAN + q * LANES : c * SPAN + (q + 1) * LANES] for c in range(chunks)], axis=1
    )


def stack(rows):
    return jnp.concatenate([lane_group(rows, q) for q in range(QUADS)], axis=0)


def interleave(groups):
    return jnp.concatenate(
        [
            group[:, c * LANES : (c + 1) * LANES]
            for c in range(groups[0].shape[1] // LANES)
            for group in groups
        ],
        axis=1,
    )


def unstack(rows, count):
    return interleave([rows[q * count : (q + 1) * count] for q in range(QUADS)])


def swap_pairs(parts):
    row = iota(parts[0].shape, 0)
    size = parts[0].shape[0]
    low = mod(row, 8) < 4
    halves = []
    for a, b in ((parts[0], parts[2]), (parts[1], parts[3])):
        halves.append(
            (
                jnp.where(low, a, pltpu.roll(b, 4, 0)),
                jnp.where(low, pltpu.roll(a, size - 4, 0), b),
            )
        )
    low = mod(row, 4) < 2
    result = []
    for side in range(2):
        a, b = halves[0][side], halves[1][side]
        result.append(jnp.where(low, a, pltpu.roll(b, 2, 0)))
        result.append(jnp.where(low, pltpu.roll(a, size - 2, 0), b))
    return result


def one_hot(condition):
    return jnp.where(condition, 1.0, 0.0).astype(jnp.bfloat16)


def select(matrix, rows):
    return jnp.dot(matrix, rows, preferred_element_type=jnp.float32)


def upright(line):
    count = line.shape[1]
    eye = iota((count, count), 0) == iota((count, count), 1)
    return jnp.sum(jnp.where(eye, line, jnp.zeros_like(line)), axis=1, keepdims=True)


def places(rows):
    tokens = rows.shape[1]
    before = iota((tokens, tokens), 1) < iota((tokens, tokens), 0)
    lying = [rows[k : k + 1, :] for k in range(TOP)]
    columns = []
    for k in range(TOP):
        col = upright(lying[k])
        same = sum(jnp.where(before & (col == line), 1, 0) for line in lying)
        place = col * CAP + jnp.sum(same, axis=1, keepdims=True)
        columns.append(jnp.concatenate([place] * QUADS, axis=0))
    return columns


def matching(shape, block_axis, tokens):
    i, j = iota(shape, block_axis), iota(shape, 1 - block_axis)
    slot = over(i, ROWS) * CAP + mod(i, CAP)
    return slot, mod(over(i, CAP), QUADS) == over(j, tokens)


def pack_matrix(columns, tokens):
    wide = QUADS * tokens
    eye = iota((wide, wide), 0) == iota((wide, wide), 1)
    slot, fits = matching((EXPERTS * ROWS, wide), 0, tokens)
    named = False
    for c in columns:
        named = named | (slot == jnp.sum(jnp.where(eye, c, 0), axis=0, keepdims=True))
    return one_hot(fits & named)


def pick_matrix(columns, tokens):
    slot, fits = matching((QUADS * tokens, EXPERTS * ROWS), 1, tokens)
    return jnp.concatenate([one_hot(fits & (slot == c)) for c in columns], axis=0)


def weight_columns(rows):
    return [jnp.concatenate([upright(rows[k : k + 1, :])] * QUADS, axis=0) for k in range(TOP)]


def kernel(
    n,
    ns,
    up_hbm,
    down_hbm,
    feed_up_hbm,
    feed_down_hbm,
    routes_hbm,
    mixing_hbm,
    gain_hbm,
    gate_hbm,
    upw_hbm,
    downw_hbm,
    out_ref,
    gate_v,
    upw_v,
    downw_v,
    send_buf,
    recv_buf,
    back_buf,
    ret_buf,
    gate_acc,
    up_acc,
    x_in,
    routes_in,
    mixing_in,
    up_ref,
    down_ref,
    feed_up_ref,
    feed_down_ref,
    routes_ref,
    mixing_ref,
    gain_ref,
    i_sem,
    w_sem,
    d_send,
    d_recv,
    r_send,
    r_recv,
    m_send,
    m_recv,
):
    me = lax.axis_index("expert")
    seg = lax.axis_index("segment")
    shards = n // EXPERTS
    small = []
    for source, target in (
        (up_hbm, up_ref),
        (down_hbm, down_ref),
        (routes_hbm, routes_ref),
        (gain_hbm, gain_ref),
        (mixing_hbm, mixing_ref),
        (feed_up_hbm, feed_up_ref),
        (feed_down_hbm, feed_down_ref),
    ):
        small.append(pltpu.make_async_copy(source, target, i_sem.at[len(small)]))
        small[-1].start()
    tokens = up_ref.shape[1]
    width = up_ref.shape[2]
    ff = gate_v.shape[1]
    tile = min(GATE_TILE, ff)
    cols = width // QUADS
    quads = n // 4
    state_refs = (up_ref, down_ref)
    feed_refs = (feed_up_ref, feed_down_ref)
    send_spans, return_spans = spans(SEND_CUTS), spans(RETURN_CUTS)

    barrier = pltpu.get_barrier_semaphore()
    for step in range(1, n):
        pl.semaphore_signal(
            barrier, inc=1, device_id={"expert": lax.rem(me + step, n)}, device_id_type=MESH
        )
    for step in (1, ns - 1):
        pl.semaphore_signal(
            barrier, inc=1, device_id={"segment": lax.rem(seg + step, ns)}, device_id_type=MESH
        )

    w_copies = []
    for lo, hi in send_spans:
        for hbm, vmem in ((gate_hbm, gate_v), (upw_hbm, upw_v)):
            at = pl.ds(lo * SPAN, (hi - lo) * SPAN)
            w_copies.append(
                pltpu.make_async_copy(hbm.at[0, at, :], vmem.at[at, :], w_sem.at[len(w_copies)])
            )
    gate_copies = len(w_copies)
    for lo, hi in return_spans:
        at = pl.ds(lo * SPAN, (hi - lo) * SPAN)
        w_copies.append(
            pltpu.make_async_copy(downw_hbm.at[0, :, at], downw_v.at[:, at], w_sem.at[len(w_copies)])
        )
    for copy in w_copies:
        copy.start()

    for copy in small:
        copy.wait()
    gain = gain_ref[...]
    gain_wide = jnp.concatenate(
        [jnp.broadcast_to(lane_group(gain, q), (tokens, cols)) for q in range(QUADS)], axis=0
    )

    def normed(values):
        squares = jnp.sum(values * values, axis=1, keepdims=True)
        total = sum(squares[q * tokens : (q + 1) * tokens] for q in range(QUADS))
        inv = lax.rsqrt(total / width + norm_eps)
        inv = jnp.concatenate([inv] * QUADS, axis=0)
        return (values * inv * gain_wide).astype(jnp.bfloat16)

    def edges(d):
        return (ns - 1, 0) if d == 0 else (0, ns - 1)

    state = [stack(ref[0].astype(jnp.float32)) for ref in state_refs]
    packs = [pack_matrix(places(routes_ref[0, d, 0]), tokens) for d in range(DIRS)]
    pending = []
    moved = []
    my_place = lax.rem(me, shards) * EXPERTS + me // shards
    for tick in range(TICKS):
        last = tick + 1 == TICKS
        for d in range(DIRS):
            packed = select(packs[d], normed(state[d]))
            for e in range(EXPERTS):
                send_buf[tick, e, d] = packed[e * ROWS : (e + 1) * ROWS].astype(jnp.bfloat16)
        if tick == 0:
            pl.semaphore_wait(barrier, n + 1)

        for g, (lo, hi) in enumerate(send_spans):
            at = pl.ds(lo * LANES, (hi - lo) * LANES)
            for step in range(1, n):
                dest = lax.rem(me + step, n)
                copy = pltpu.make_async_remote_copy(
                    src_ref=send_buf.at[tick, dest // shards, :, :, at],
                    dst_ref=recv_buf.at[tick, me, :, :, at],
                    send_sem=d_send.at[tick, g, step],
                    recv_sem=d_recv.at[tick, g, me],
                    device_id={"expert": dest},
                    device_id_type=MESH,
                )
                copy.start()
                pending.append(copy)
        recv_buf[tick, me] = send_buf[tick, me // shards]

        if not last:
            for d in range(DIRS):
                edge_out, edge_in = edges(d)
                ahead = 1 if d == 0 else ns - 1
                sources = (state_refs[d].at[0], routes_ref.at[tick, d, 0], mixing_ref.at[tick, d, 0])
                for a, (source, target) in enumerate(zip(sources, (x_in, routes_in, mixing_in))):
                    copy = pltpu.make_async_remote_copy(
                        src_ref=source,
                        dst_ref=target.at[d],
                        send_sem=m_send.at[d, a],
                        recv_sem=m_recv.at[d, a],
                        device_id={"segment": lax.rem(seg + ahead, ns)},
                        device_id_type=MESH,
                    )

                    @pl.when(seg != edge_out)
                    def _():
                        copy.start()

                    moved.append((copy, edge_out, edge_in))

                @pl.when(seg == edge_in)
                def _():
                    x_in[d] = feed_refs[d][tick]
                    routes_in[d] = routes_ref[tick, d, 0]
                    mixing_in[d] = mixing_ref[tick, d, 0]

            packs = [pack_matrix(places(routes_ref[tick + 1, d, 0]), tokens) for d in range(DIRS)]
        else:
            picks = [pick_matrix(places(routes_ref[tick, d, 0]), tokens) for d in range(DIRS)]
            weights = [weight_columns(mixing_ref[tick, d, 0]) for d in range(DIRS)]

        for g, (lo, hi) in enumerate(send_spans):
            at = pl.ds(lo * LANES, (hi - lo) * LANES)
            for step in range(1, n):
                source = lax.rem(me + n - step, n)
                pltpu.make_async_remote_copy(
                    src_ref=send_buf.at[tick, 0, :, :, at],
                    dst_ref=recv_buf.at[tick, source, :, :, at],
                    send_sem=d_send.at[tick, g, step],
                    recv_sem=d_recv.at[tick, g, source],
                    device_id={"expert": source},
                    device_id_type=MESH,
                ).wait_recv()
            parts = [
                jnp.concatenate(
                    [
                        recv_buf[tick, 4 * i + j, d, :, lo * LANES : hi * LANES].astype(jnp.float32)
                        for d in range(DIRS)
                        for i in range(quads)
                    ],
                    axis=0,
                )
                for j in range(4)
            ]
            lhs = interleave([p.astype(jnp.bfloat16) for p in swap_pairs(parts)])
            if tick == 0:
                w_copies[2 * g].wait()
                w_copies[2 * g + 1].wait()
            for f in range(ff // tile):
                at = slice(f * tile, (f + 1) * tile)
                deep = slice(lo * SPAN, hi * SPAN)
                for weight, acc in ((gate_v, gate_acc), (upw_v, up_acc)):
                    value = jnp.dot(lhs, weight[deep, at], preferred_element_type=jnp.float32)
                    if g:
                        value = acc[:, at] + value
                    acc[:, at] = value
        hidden = (jax.nn.silu(gate_acc[...]) * up_acc[...]).astype(jnp.bfloat16)

        for r, (lo, hi) in enumerate(return_spans):
            if tick == 0:
                w_copies[gate_copies + r].wait()
            piece = jnp.dot(
                hidden, downw_v[:, lo * SPAN : hi * SPAN], preferred_element_type=jnp.float32
            )
            parts = swap_pairs([lane_group(piece, q) for q in range(QUADS)])
            for j in range(4):
                for d in range(DIRS):
                    for i in range(quads):
                        row = (d * quads + i) * 8
                        back_buf[tick, 4 * i + j, d, :, lo * LANES : hi * LANES] = parts[j][
                            row : row + 8
                        ].astype(jnp.bfloat16)
            at = pl.ds(lo * LANES, (hi - lo) * LANES)
            if last:
                for step in range(1, n):
                    dest = lax.rem(me + step, n)
                    copy = pltpu.make_async_remote_copy(
                        src_ref=back_buf.at[tick, dest, :, :, at],
                        dst_ref=ret_buf.at[tick, my_place, :, :, at],
                        send_sem=r_send.at[tick, r, 0, step],
                        recv_sem=r_recv.at[tick, r, 0, my_place],
                        device_id={"expert": dest},
                        device_id_type=MESH,
                    )
                    copy.start()
                    pending.append(copy)
                ret_buf[tick, my_place, :, :, lo * LANES : hi * LANES] = back_buf[
                    tick, me, :, :, lo * LANES : hi * LANES
                ]
            else:
                for d in range(DIRS):
                    edge_out, edge_in = edges(d)
                    ahead = 1 if d == 0 else ns - 1
                    batch = []
                    for step in range(n):
                        dest = lax.rem(me + step, n)
                        copy = pltpu.make_async_remote_copy(
                            src_ref=back_buf.at[tick, dest, d, :, at],
                            dst_ref=ret_buf.at[tick, my_place, d, :, at],
                            send_sem=r_send.at[tick, r, d, step],
                            recv_sem=r_recv.at[tick, r, d, my_place],
                            device_id={"segment": lax.rem(seg + ahead, ns), "expert": dest},
                            device_id_type=MESH,
                        )
                        batch.append(copy)
                        moved.append((copy, edge_out, None))

                    @pl.when(seg != edge_out)
                    def _():
                        for copy in batch:
                            copy.start()

        if not last:
            for d in range(DIRS):

                @pl.when(seg != edges(d)[1])
                def _():
                    for copy, edge_out, edge_in in moved:
                        if edge_in == edges(d)[1]:
                            copy.wait_recv()

            picks = [pick_matrix(places(routes_in[d]), tokens) for d in range(DIRS)]
            weights = [weight_columns(mixing_in[d]) for d in range(DIRS)]
            state = [stack(x_in[d].astype(jnp.float32)) for d in range(DIRS)]

        results = [[] for _ in range(DIRS)]
        for r, (lo, hi) in enumerate(return_spans):
            at = pl.ds(lo * LANES, (hi - lo) * LANES)

            def arrived(d, step):
                source = lax.rem(me + n - step, n)
                place = lax.rem(source, shards) * EXPERTS + source // shards
                which = slice(None) if last else d
                pltpu.make_async_remote_copy(
                    src_ref=back_buf.at[tick, 0, which, :, at],
                    dst_ref=ret_buf.at[tick, place, which, :, at],
                    send_sem=r_send.at[tick, r, d, step],
                    recv_sem=r_recv.at[tick, r, d, place],
                    device_id={"expert": source},
                    device_id_type=MESH,
                ).wait_recv()

            if last:
                for step in range(1, n):
                    arrived(0, step)
            else:
                for d in range(DIRS):

                    @pl.when(seg != edges(d)[1])
                    def _():
                        for step in range(n):
                            arrived(d, step)

            for d in range(DIRS):
                total = None
                for s in range(shards):
                    block = jnp.concatenate(
                        [
                            ret_buf[tick, s * EXPERTS + e, d, :, lo * LANES : hi * LANES].astype(
                                jnp.float32
                            )
                            for e in range(EXPERTS)
                        ],
                        axis=0,
                    )
                    if not last:
                        block = jnp.where(seg == edges(d)[1], 0.0, block)
                    found = select(picks[d], block.astype(jnp.bfloat16))
                    total = found if total is None else total + found
                wide = QUADS * tokens
                mixed = total[:wide] * weights[d][0] + total[wide:] * weights[d][1]
                old = state[d][:, lo * LANES : hi * LANES]
                results[d].append(old + mixed)
        state = [jnp.concatenate(r, axis=1).astype(jnp.bfloat16) for r in results]
        if last:
            for d in range(DIRS):
                out_ref[d] = unstack(state[d].astype(jnp.float32), tokens).astype(jnp.bfloat16)
        else:
            state = [s.astype(jnp.float32) for s in state]

    for copy in pending:
        copy.wait_send()
    for d in range(DIRS):

        @pl.when(seg != edges(d)[0])
        def _():
            for copy, edge_out, _ in moved:
                if edge_out == edges(d)[0]:
                    copy.wait_send()


def body(
    state_up,
    state_down,
    feed_up,
    feed_down,
    routes,
    mixing,
    norm_gain,
    gate_weight,
    up_weight,
    down_weight,
):
    n = lax.axis_size("expert")
    ns = lax.axis_size("segment")
    _, tokens, width = state_up.shape
    ff = gate_weight.shape[2]
    cols = width // QUADS
    sends, parts = len(SEND_CUTS) - 1, len(RETURN_CUTS) - 1
    bf16 = jnp.bfloat16
    vmem = pl.BlockSpec(memory_space=pltpu.VMEM)
    hbm = pl.BlockSpec(memory_space=pl.ANY)
    dma = pltpu.SemaphoreType.DMA
    swapped = jnp.swapaxes(routes, 3, 4)
    both = pl.pallas_call(
        functools.partial(kernel, n, ns),
        out_shape=jax.ShapeDtypeStruct((DIRS, tokens, width), bf16),
        in_specs=[hbm] * 10,
        out_specs=vmem,
        scratch_shapes=[
            pltpu.VMEM((width, ff), bf16),
            pltpu.VMEM((width, ff), bf16),
            pltpu.VMEM((ff, width), bf16),
            pltpu.VMEM((TICKS, EXPERTS, DIRS, ROWS, cols), bf16),
            pltpu.VMEM((TICKS, n, DIRS, ROWS, cols), bf16),
            pltpu.VMEM((TICKS, n, DIRS, ROWS, cols), bf16),
            pltpu.VMEM((TICKS, n, DIRS, ROWS, cols), bf16),
            pltpu.VMEM((n * DIRS * CAP, ff), jnp.float32),
            pltpu.VMEM((n * DIRS * CAP, ff), jnp.float32),
            pltpu.VMEM((DIRS, tokens, width), bf16),
            pltpu.VMEM((DIRS, TOP, tokens), jnp.int32),
            pltpu.VMEM((DIRS, TOP, tokens), jnp.float32),
            pltpu.VMEM(state_up.shape, bf16),
            pltpu.VMEM(state_down.shape, bf16),
            pltpu.VMEM(feed_up.shape, bf16),
            pltpu.VMEM(feed_down.shape, bf16),
            pltpu.VMEM(swapped.shape, jnp.int32),
            pltpu.VMEM(swapped.shape, jnp.float32),
            pltpu.VMEM(norm_gain.shape, jnp.float32),
            dma((7,)),
            dma((2 * sends + parts,)),
            dma((TICKS, sends, n)),
            dma((TICKS, sends, n)),
            dma((TICKS, parts, DIRS, n)),
            dma((TICKS, parts, DIRS, n)),
            dma((DIRS, 3)),
            dma((DIRS, 3)),
        ],
        compiler_params=pltpu.CompilerParams(collective_id=0, has_side_effects=True),
    )(
        state_up,
        state_down,
        feed_up,
        feed_down,
        swapped,
        jnp.swapaxes(mixing, 3, 4),
        norm_gain,
        gate_weight,
        up_weight,
        down_weight,
    )
    return both[0:1], both[1:2]


def solution(mesh):
    placed = (
        P("segment", "expert", None),
        P("segment", "expert", None),
        P(None, "expert", None),
        P(None, "expert", None),
        P(None, None, "segment", "expert", None),
        P(None, None, "segment", "expert", None),
        P("segment", None),
        P("segment", None, "expert"),
        P("segment", None, "expert"),
        P("segment", "expert", None),
    )
    return jax.shard_map(
        body,
        mesh=mesh,
        in_specs=placed,
        out_specs=(P("segment", "expert", None), P("segment", "expert", None)),
        check_vma=False,
    )
```
